512 devices in a mesh: seq: 64 (over z_hi, y, x), head: 8 (over z_lo, core).
Axes of the slice: x: 4, y: 8, z: 8 (z_hi: 2, z_lo: 4; z = z_hi * 4 + z_lo), core: 2. Of those that a mesh axis runs over, the one named last changes fastest.
Arguments:
- queries: bfloat16 [16384, 4096], P('seq', 'head'), may hold values from -6 to 6
- key_rows: bfloat16 [16384, 4096], P('seq', 'head'), may hold values from -6 to 6
- value_rows: bfloat16 [16384, 4096], P('seq', 'head'), may hold values from -180 to 180
- window: int32 [256, 12], P('seq'), may hold values from 0 to 255, as said below
- random_blocks: int32 [256, 3], P('seq'), may hold values from 0 to 255, as said below
- global_blocks: int32 [2], replicated, may hold values from 0 to 255, as said below
- norm_gain: float32 [4096], P('head'), may hold values from 0.25 to 1.75
Outputs:
- normed: bfloat16 [16384, 4096], P('seq', 'head')
The draws below stay inside these ranges and needn't reach their ends.
Inputs may be any that keep to these rules, and one draw needn't show every extreme that they name: `window`: row b names 12 distinct blocks, each with (id - b) mod 256 within 8 of 0 either way around the circle; b itself, b - 8 and b + 8 (mod 256) are always among them. `random_blocks`: shard s holds blocks s * 4 to s * 4 + 3. The 12 entries of the rows of one device name each shard at most 1 times; one shard is named exactly 1 times by the rows of every device. `global_blocks`: distinct blocks; one of them is the last block of the sequence, 255.
All inputs are finite; a program needn't handle non-finite values.
Results may differ from the reference program's by a relative error of at most 0.0045.
Values may be sent and summed in bfloat16 or wider, within the bound.
A program may use at most 128 MiB of HBM per device.

```python
import math
import jax
import jax.numpy as jnp
from jax import lax

HEADS = 32
HD = 128
D = 4096
BLK = 64
BLK_DEV = 4
RAND = 3
SEQ = 16384
NBLK = 256
REACH = 8
WIN = 12
SLOTS = 1


def draw_queries(key, part):
    base = jnp.clip(jax.random.normal(jax.random.fold_in(key, 1), (SEQ, D), jnp.float32), -6.0, 6.0)
    return base.astype(jnp.bfloat16)


def draw_key_rows(key, part):
    base = jnp.clip(jax.random.normal(jax.random.fold_in(key, 2), (SEQ, D), jnp.float32), -6.0, 6.0)
    return base.astype(jnp.bfloat16)


def draw_value_rows(key, part):
    head_of = (jnp.arange(D, dtype=jnp.int32) // HD).astype(jnp.float32)
    spread = head_of / max(HEADS - 1, 1)
    row_scale = jnp.exp(jax.random.uniform(jax.random.fold_in(key, 5), (SEQ, 1), jnp.float32, 0.0, math.log(10.0)))
    base = jnp.clip(jax.random.normal(jax.random.fold_in(key, 4), (SEQ, D), jnp.float32), -6.0, 6.0)
    column_scale = 1.0 + 2.0 * spread
    return (base * column_scale[None, :] * row_scale).astype(jnp.bfloat16)


def draw_window(key, part):
    middle = jnp.concatenate([jnp.arange(-REACH + 1, 0), jnp.arange(1, REACH)]).astype(jnp.int32)
    pick_keys = jax.random.split(jax.random.fold_in(key, 1), NBLK)
    picked = jax.vmap(lambda one_key: jax.random.permutation(one_key, middle)[:WIN - 3])(pick_keys)
    edges = jnp.broadcast_to(jnp.array([0, -REACH, REACH], dtype=jnp.int32), (NBLK, 3))
    offsets = jnp.concatenate([edges, picked.astype(jnp.int32)], axis=1)
    order_keys = jax.random.split(jax.random.fold_in(key, 2), NBLK)
    orders = jax.vmap(lambda one_key: jax.random.permutation(one_key, WIN))(order_keys)
    offsets = jnp.take_along_axis(offsets, orders, axis=1)
    block_ids = jnp.arange(NBLK, dtype=jnp.int32)[:, None]
    return ((block_ids + offsets) % NBLK).astype(jnp.int32)


def draw_random_blocks(key, part):
    used_count = BLK_DEV * RAND
    slot_total = NBLK // BLK_DEV * SLOTS
    shard_total = NBLK // BLK_DEV
    common_shard = jax.random.randint(jax.random.fold_in(key, 1), (), 0, shard_total)
    owner_keys = jax.random.split(jax.random.fold_in(key, 2), shard_total)
    shuffled = jax.vmap(lambda one_key: jax.random.permutation(one_key, slot_total))(owner_keys).astype(jnp.int32)
    shard_of = shuffled // SLOTS
    grouping = jnp.where(shard_of == common_shard, 0, 1).astype(jnp.int32)
    ordering = jnp.argsort(grouping, axis=1, stable=True)
    chosen = jnp.take_along_axis(shard_of, ordering, axis=1)[:, :used_count]
    mix_keys = jax.random.split(jax.random.fold_in(key, 3), shard_total)
    mixing = jax.vmap(lambda one_key: jax.random.permutation(one_key, used_count))(mix_keys)
    chosen = jnp.take_along_axis(chosen, mixing, axis=1)
    within = jax.random.randint(jax.random.fold_in(key, 4), (shard_total, used_count), 0, BLK_DEV)
    return (chosen * BLK_DEV + within).reshape(NBLK, RAND).astype(jnp.int32)


def draw_global_blocks(key, part):
    other_block = jax.random.randint(jax.random.fold_in(key, 1), (), 0, NBLK - 1).astype(jnp.int32)
    last_block = jnp.array(NBLK - 1, dtype=jnp.int32)
    flipped = jax.random.randint(jax.random.fold_in(key, 2), (), 0, 2).astype(jnp.int32)
    first = jnp.where(flipped == 1, other_block, last_block)
    second = jnp.where(flipped == 1, last_block, other_block)
    return jnp.stack([first, second]).astype(jnp.int32)


def setup_inputs(seed: int = 0) -> dict:
    key_list = jax.random.split(jax.random.key(seed), 8)
    queries = draw_queries(jax.random.fold_in(key_list[7], 71), 0)
    key_rows = draw_key_rows(jax.random.fold_in(key_list[7], 71), 0)
    value_rows = draw_value_rows(jax.random.fold_in(key_list[7], 71), 0)
    window = draw_window(jax.random.fold_in(key_list[7], 71), 0)
    random_blocks = draw_random_blocks(jax.random.fold_in(key_list[7], 71), 0)
    global_blocks = draw_global_blocks(jax.random.fold_in(key_list[7], 71), 0)
    norm_gain = jnp.clip(1.0 + 0.15 * jax.random.normal(key_list[6], (D,), jnp.float32), 0.25, 1.75)
    return dict(queries=queries, key_rows=key_rows, value_rows=value_rows, window=window, random_blocks=random_blocks, global_blocks=global_blocks, norm_gain=norm_gain)


def source_part(query_set, key_set, value_set, head_count):
    item_count, row_count, row_width = query_set.shape
    head_size = row_width // head_count
    query_heads = query_set.reshape(item_count, row_count, head_count, head_size).astype(jnp.float32)
    key_heads = key_set.reshape(item_count, key_set.shape[1], head_count, head_size).astype(jnp.float32)
    value_heads = value_set.reshape(item_count, value_set.shape[1], head_count, head_size).astype(jnp.float32)
    scores = jnp.einsum('nqhd,nkhd->nhqk', query_heads, key_heads) * head_size ** (-0.5)
    maxima = lax.optimization_barrier(jnp.max(scores, axis=-1))
    lifted = jnp.exp(scores - maxima[..., None])
    totals = lax.optimization_barrier(jnp.sum(lifted, axis=-1))
    weights = lax.optimization_barrier(lifted.astype(jnp.bfloat16)).astype(jnp.float32)
    summed = jnp.einsum('nhqk,nkhd->nqhd', weights, value_heads)
    return (maxima, totals, summed.reshape(item_count, row_count, row_width))

def merge_sources(maxima, totals, partial_sums, head_count):
    overall = lax.optimization_barrier(jnp.max(maxima, axis=0))
    factor = jnp.exp(maxima - overall[None])
    denominator = lax.optimization_barrier(jnp.sum(factor * totals, axis=0))
    item_count, row_count, row_width = partial_sums.shape
    split_sums = partial_sums.reshape(item_count, row_count, head_count, row_width // head_count)
    weighted = lax.optimization_barrier(jnp.sum(split_sums * jnp.transpose(factor, (0, 2, 1))[..., None], axis=0))
    return (weighted / jnp.transpose(denominator)[..., None]).reshape(row_count, row_width)

def reference(queries, key_rows, value_rows, window, random_blocks, global_blocks, norm_gain):
    row_width = queries.shape[1]
    head_count = row_width // HD
    query_blocks = queries.reshape(NBLK, BLK, row_width)
    key_blocks = key_rows.reshape(NBLK, BLK, row_width)
    value_blocks = value_rows.reshape(NBLK, BLK, row_width)

    def one_block(block_id):
        one_query = lax.dynamic_index_in_dim(query_blocks, block_id, 0, keepdims=True)
        near_ids = jnp.concatenate([lax.dynamic_index_in_dim(window, block_id, 0, keepdims=False).astype(jnp.int32), global_blocks.astype(jnp.int32)])
        near_keys = jnp.take(key_blocks, near_ids, axis=0).reshape(1, -1, row_width)
        near_values = jnp.take(value_blocks, near_ids, axis=0).reshape(1, -1, row_width)
        near_max, near_total, near_sum = source_part(one_query, near_keys, near_values, head_count)
        rand_ids = lax.dynamic_index_in_dim(random_blocks, block_id, 0, keepdims=False).astype(jnp.int32)
        rand_keys = jnp.take(key_blocks, rand_ids, axis=0)
        rand_values = jnp.take(value_blocks, rand_ids, axis=0)
        repeated = jnp.broadcast_to(one_query, (rand_ids.shape[0], BLK, row_width))
        rand_max, rand_total, rand_sum = source_part(repeated, rand_keys, rand_values, head_count)
        return merge_sources(jnp.concatenate([near_max, rand_max]), jnp.concatenate([near_total, rand_total]), jnp.concatenate([near_sum, rand_sum]), head_count)
    attended = lax.map(one_block, jnp.arange(NBLK, dtype=jnp.int32)).reshape(SEQ, row_width)
    row_squares = lax.optimization_barrier(jnp.sum(attended * attended, axis=1))
    inverse = lax.rsqrt(row_squares / D + 1e-06)
    return (attended * inverse[:, None] * norm_gain[None, :]).astype(jnp.bfloat16)
```

```python
from functools import partial

import jax
import jax.numpy as jnp
from jax import lax
from jax.experimental import pallas as pl
from jax.experimental.pallas import tpu as pltpu
from jax.sharding import PartitionSpec as P

HD = 128
D = 4096
BLK = 64
NX, NY, NZ = 4, 8, 2
SHARDS = NX * NY * NZ
PER = 4
RANDS = 12
SLOTS = 14
HALF = 7
WIN = 12
MESH = pl.DeviceIdType.MESH


def exchange_kernel(ids_ref, k_ref, v_ref, near_ref, sel_ref,
                    key_col, value_col, out_buf, in_buf, ids_all, ids_smem,
                    own_sem, id_send, id_recv, z_send, z_recv, w_send, w_recv,
                    y_send, y_recv, x_send, x_recv, smem_sem):
    s = lax.axis_index("seq")
    mx = lax.rem(s, NX)
    my = lax.rem(s // NX, NY)
    mz = s // (NX * NY)
    kv = (k_ref, v_ref)
    col = (key_col, value_col)

    def at(z, y, x):
        return z * (NX * NY) + y * NX + x

    def wrap(value, size):
        return lax.rem(value + 2 * size, size)

    z_peer = at(1 - mz, my, mx)
    y_peer = (at(mz, wrap(my + 1, NY), mx), at(mz, wrap(my - 1, NY), mx))
    x_peer = [at(mz, my, wrap(mx + i, NX)) for i in range(NX)]
    w_peer = {o: wrap(s + o, SHARDS) for o in (-2, -1, 1, 2)}

    def remote(src, dst, send, recv, to):
        return pltpu.make_async_remote_copy(
            src_ref=src, dst_ref=dst, send_sem=send, recv_sem=recv,
            device_id={"seq": to}, device_id_type=MESH)

    barrier = pltpu.get_barrier_semaphore()
    greeted = [z_peer, *y_peer, *x_peer[1:], *w_peer.values()]
    for peer in greeted:
        pl.semaphore_signal(barrier, inc=1, device_id={"seq": peer}, device_id_type=MESH)
    own = [pltpu.make_async_copy(kv[c], col[c].at[0, my], own_sem.at[c]) for c in range(2)]
    own_ids = pltpu.make_async_copy(ids_ref, ids_all.at[mx], own_sem.at[2])
    for copy in own:
        copy.start()
    own_ids.start()
    pl.semaphore_wait(barrier, len(greeted))

    sends = []

    def y_copy(zz, c, way, t, y_src):
        part = pl.ds(0, PER) if t < 4 else pl.ds(2 * way, 2)
        block = col[c].at[zz, y_src, part]
        if t == 1 and zz == 0:
            source = kv[c]
        else:
            source = block
        return remote(source, block, y_send.at[zz, c, way, t - 1],
                      y_recv.at[zz, c, way, t - 1], y_peer[way])

    def y_start(zz, c, t):
        for way, sign in ((0, 1), (1, -1)):
            copy = y_copy(zz, c, way, t, wrap(my - sign * (t - 1), NY))
            copy.start()
            sends.append(copy)

    def y_wait(zz, c, t, way):
        sign = 1 - 2 * way
        y_copy(zz, c, way, t, wrap(my - sign * t, NY)).wait_recv()

    z_copies = [remote(kv[c], col[c].at[1, my], z_send.at[c], z_recv.at[c], z_peer)
                for c in range(2)]

    def y_phase(zz, c, t):
        if t == 0:
            if zz == 1:
                z_copies[c].wait_recv()
            y_start(zz, c, 1)
        elif t < 4:
            for way in range(2):
                y_wait(zz, c, t, way)
            y_start(zz, c, t + 1)
        else:
            for way in range(2):
                y_wait(zz, c, 4, way)

    def x_copy(c, way, i):
        to = x_peer[1] if way == 0 else x_peer[3]
        return remote(out_buf.at[c, way, i], in_buf.at[c, way, i], x_send.at[c, way, i],
                      x_recv.at[c, way, i], to)

    def x_phase(c, i):
        for way in range(2):
            away = (3 - i) if way == 0 else (1 + i)
            dest = wrap(mx + away, NX)
            if i == 3:
                dest = mx
            if i > 0:
                x_copy(c, way, i - 1).wait_recv()

            def fill(j, carry, way=way, dest=dest):
                slot = j + way * HALF
                block_id = ids_smem[dest, 0, slot]
                shard = block_id // PER
                picked = col[c][jnp.where(shard // (NX * NY) == mz, 0, 1),
                                lax.rem(shard // NX, NY), lax.rem(block_id, PER)]
                if i > 0:
                    mine = lax.rem(shard, NX) == mx
                    picked = lax.select(mine, picked, in_buf[c, way, i - 1, j])
                if i == 3:
                    sel_ref[c, slot] = picked
                else:
                    out_buf[c, way, i, j] = picked
                return carry

            lax.fori_loop(0, HALF, fill, 0)
            if i < 3:
                copy = x_copy(c, way, i)
                copy.start()
                sends.append(copy)

    y_phase(0, 0, 0)
    for copy in z_copies:
        copy.start()
    own_ids.wait()
    id_copies = []
    for i in (1, 2, 3):
        copy = remote(ids_ref, ids_all.at[mx], id_send.at[i - 1], id_recv.at[i - 1], x_peer[i])
        copy.start()
        id_copies.append(copy)
    near_copies = []
    for n, o in enumerate((1, -1, 2, -2)):
        for c in range(2):
            copy = remote(kv[c], near_ref.at[2 - o, c], w_send.at[n, c], w_recv.at[n, c], w_peer[o])
            copy.start()
            near_copies.append(copy)
    for copy in own:
        copy.wait()
    keep_own = [pltpu.make_async_copy(col[c].at[0, my], near_ref.at[2, c], own_sem.at[3 + c])
                for c in range(2)]
    for copy in keep_own:
        copy.start()

    begin = {(0, 0): 0, (1, 0): 3, (0, 1): 6, (1, 1): 9}
    x_at = {8: (0, 0), 9: (0, 1), 11: (0, 2), 13: (0, 3)}
    for tick in range(1, 14):
        for (zz, c), first in begin.items():
            t = tick - first
            if 0 <= t <= 4:
                y_phase(zz, c, t)
        if tick == 7:
            for i in (1, 2, 3):
                remote(ids_ref, ids_all.at[wrap(mx - i, NX)], id_send.at[i - 1],
                       id_recv.at[i - 1], x_peer[i]).wait_recv()
            to_smem = pltpu.make_async_copy(ids_all, ids_smem, smem_sem)
            to_smem.start()
            to_smem.wait()
        if tick in x_at:
            x_phase(*x_at[tick])
    for i in range(4):
        x_phase(1, i)

    for copy in keep_own:
        copy.wait()
    for copy in near_copies:
        copy.wait_recv()
    for copy in near_copies + id_copies + z_copies + sends:
        copy.wait_send()


def exchange(ids, keys, values):
    width = keys.shape[-1]
    dma = pltpu.SemaphoreType.DMA
    hbm = pl.BlockSpec(memory_space=pl.ANY)
    vmem = pl.BlockSpec(memory_space=pltpu.VMEM)
    return pl.pallas_call(
        exchange_kernel,
        out_shape=(jax.ShapeDtypeStruct((5, 2, PER, BLK, width), jnp.bfloat16),
                   jax.ShapeDtypeStruct((2, SLOTS, BLK, width), jnp.bfloat16)),
        in_specs=[vmem, hbm, hbm],
        out_specs=(hbm, vmem),
        scratch_shapes=[
            pltpu.VMEM((2, NY, PER, BLK, width), jnp.bfloat16),
            pltpu.VMEM((2, NY, PER, BLK, width), jnp.bfloat16),
            pltpu.VMEM((2, 2, 3, HALF, BLK, width), jnp.bfloat16),
            pltpu.VMEM((2, 2, 3, HALF, BLK, width), jnp.bfloat16),
            pltpu.VMEM((NX, 8, 128), jnp.int32),
            pltpu.SMEM((NX, 8, 128), jnp.int32),
            dma((5,)), dma((3,)), dma((3,)), dma((2,)), dma((2,)), dma((4, 2)), dma((4, 2)),
            dma((2, 2, 2, 4)), dma((2, 2, 2, 4)), dma((2, 2, 3)), dma((2, 2, 3)), dma(()),
        ],
        compiler_params=pltpu.CompilerParams(
            collective_id=0, has_side_effects=True, vmem_limit_bytes=48 << 20),
        name="exchange",
    )(ids, keys, values)


def attend_kernel(win_ref, q_ref, near_ref, sel_ref, out_ref, key_buf, value_buf):
    b = pl.program_id(0)
    s = lax.axis_index("seq")
    for j in range(WIN):
        block_id = win_ref[b, j]
        o = lax.rem(block_id // PER - s + 2 + SHARDS, SHARDS)
        w = lax.rem(block_id, PER)
        rows = pl.ds(j * BLK, BLK)
        key_buf[rows, :] = near_ref[o, 0, w]
        value_buf[rows, :] = near_ref[o, 1, w]
    for r in range(5):
        slot = b * 3 + r if r < 3 else RANDS + r - 3
        rows = pl.ds((WIN + r) * BLK, BLK)
        key_buf[rows, :] = sel_ref[0, slot]
        value_buf[rows, :] = sel_ref[1, slot]
    for h in range(q_ref.shape[-1] // HD):
        lanes = slice(h * HD, (h + 1) * HD)
        scores = lax.dot_general(q_ref[0, :, lanes], key_buf[:, lanes], (((1,), (1,)), ((), ())),
                                 preferred_element_type=jnp.float32)
        peak = jnp.max(scores, axis=-1, keepdims=True)
        lifted = jnp.exp((scores - peak) * HD ** -0.5)
        total = jnp.sum(lifted, axis=-1, keepdims=True)
        part = jnp.dot(lifted.astype(jnp.bfloat16), value_buf[:, lanes],
                       preferred_element_type=jnp.float32)
        out_ref[0, :, lanes] = part / total


def attend(window, queries, near, sel):
    width = queries.shape[-1]
    keys_total = (WIN + 5) * BLK
    whole = lambda shape: pl.BlockSpec(shape, lambda b, *_: (0,) * len(shape),
                                       pipeline_mode=pl.Buffered(1))
    return pl.pallas_call(
        attend_kernel,
        out_shape=jax.ShapeDtypeStruct((PER, BLK, width), jnp.float32),
        grid_spec=pltpu.PrefetchScalarGridSpec(
            num_scalar_prefetch=1, grid=(PER,),
            in_specs=[pl.BlockSpec((1, BLK, width), lambda b, *_: (b, 0, 0)),
                      whole(near.shape), whole(sel.shape)],
            out_specs=pl.BlockSpec((1, BLK, width), lambda b, *_: (b, 0, 0)),
            scratch_shapes=[pltpu.VMEM((keys_total, width), jnp.bfloat16),
                            pltpu.VMEM((keys_total, width), jnp.bfloat16)]),
        compiler_params=pltpu.CompilerParams(vmem_limit_bytes=48 << 20),
        name="attend",
    )(window, queries, near, sel)


def body(queries, key_rows, value_rows, window, random_blocks, global_blocks, norm_gain):
    width = queries.shape[1]
    blocks = lambda rows: rows.reshape(PER, BLK, width)
    ids = jnp.concatenate([random_blocks.reshape(-1), global_blocks])
    ids = jnp.broadcast_to(jnp.pad(ids, (0, 128 - SLOTS))[None, :], (8, 128))
    near, sel = exchange(ids, blocks(key_rows), blocks(value_rows))
    attended = attend(window, blocks(queries), near, sel).reshape(-1, width)
    row_squares = jnp.sum(attended * attended, axis=1)
    all_squares = lax.psum(row_squares, "head")
    inverse = lax.rsqrt(all_squares / D + 1e-06)
    return (attended * inverse[:, None] * norm_gain[None, :]).astype(jnp.bfloat16)


def solution(mesh):
    placed = (
        P("seq", "head"),
        P("seq", "head"),
        P("seq", "head"),
        P("seq", None),
        P("seq", None),
        P(),
        P("head"),
    )
    return jax.shard_map(
        body, mesh=mesh, in_specs=placed, out_specs=P("seq", "head"), check_vma=False
    )
```

```python
from functools import partial

import jax
import jax.numpy as jnp
from jax import lax
from jax.experimental import pallas as pl
from jax.experimental.pallas import tpu as pltpu
from jax.sharding import PartitionSpec as P

HD = 128
D = 4096
BLK = 64
NX, NY, NZ = 4, 8, 2
SHARDS = NX * NY * NZ
PER = 4
RANDS = 12
SLOTS = 14
HALF = 7
WIN = 12
SPLIT = 2
GROUPS = 2 * SPLIT
LANES = 512 // SPLIT
FIRST, X_LAG, X_GAP = 3, 5, 2
MESH = pl.DeviceIdType.MESH


def remote_copy(src, dst, send, recv, axis, to):
    return pltpu.make_async_remote_copy(
        src_ref=src, dst_ref=dst, send_sem=send, recv_sem=recv,
        device_id={axis: to}, device_id_type=MESH)


def greet(axis, peers):
    barrier = pltpu.get_barrier_semaphore()
    for peer in peers:
        pl.semaphore_signal(barrier, inc=1, device_id={axis: peer}, device_id_type=MESH)
    return lambda: pl.semaphore_wait(barrier, len(peers))


def exchange_kernel(ids_ref, k_ref, v_ref, near_ref, sel_ref, *scratch):
    col = scratch[:GROUPS]
    (out_buf, in_buf, ids_all, ids_smem, own_sem, keep_sem, id_send, id_recv, z_send, z_recv,
     w_send, w_recv, y_send, y_recv, x_send, x_recv, smem_sem) = scratch[GROUPS:]
    s = lax.axis_index("seq")
    mx = lax.rem(s, NX)
    my = lax.rem(s // NX, NY)
    mz = s // (NX * NY)
    remote = partial(remote_copy, axis="seq")

    def lanes(g):
        return pl.ds((g % SPLIT) * LANES, LANES)

    own_kv = [(k_ref, v_ref)[g // SPLIT].at[:, :, lanes(g)] for g in range(GROUPS)]

    def at(z, y, x):
        return z * (NX * NY) + y * NX + x

    def wrap(value, size):
        return lax.rem(value + 2 * size, size)

    z_peer = at(1 - mz, my, mx)
    y_peer = (at(mz, wrap(my + 1, NY), mx), at(mz, wrap(my - 1, NY), mx))
    x_peer = [at(mz, my, wrap(mx + i, NX)) for i in range(NX)]

    await_peers = greet("seq", [z_peer, *y_peer, *x_peer[1:]])
    own = [pltpu.make_async_copy(own_kv[g], col[g].at[0, my], own_sem.at[g]) for g in range(GROUPS)]
    own_ids = pltpu.make_async_copy(ids_ref, ids_all.at[mx], smem_sem.at[0])
    for copy in own:
        copy.start()
    own_ids.start()
    await_peers()

    sends = []

    def begin(copy):
        copy.start()
        sends.append(copy)

    def y_copy(zz, g, way, t, y_src):
        part = pl.ds(0, PER) if t < 4 else pl.ds(2 * way, 2)
        block = col[g].at[zz, y_src, part]
        source = own_kv[g] if t == 1 and zz == 0 else block
        return remote(source, block, y_send.at[zz, g, way, t - 1],
                      y_recv.at[zz, g, way, t - 1], to=y_peer[way])

    def y_start(zz, g, t):
        for way, sign in ((0, 1), (1, -1)):
            begin(y_copy(zz, g, way, t, wrap(my - sign * (t - 1), NY)))

    def y_wait(zz, g, t):
        for way, sign in ((0, 1), (1, -1)):
            y_copy(zz, g, way, t, wrap(my - sign * t, NY)).wait_recv()

    z_copies = [remote(own_kv[g], col[g].at[1, my], z_send.at[g], z_recv.at[g], to=z_peer)
                for g in range(GROUPS)]

    def y_phase(zz, g, t):
        if t == 0:
            if zz == 1:
                z_copies[g].wait_recv()
        else:
            y_wait(zz, g, t)
        if t < 4:
            y_start(zz, g, t + 1)

    def w_copy(g, n):
        away, o = ((1, -1), (-1, 1), (2, 2), (2, -2))[n]
        to = x_peer[away % NX]
        shard = wrap(to + o, SHARDS)
        block = col[g].at[jnp.where(shard // (NX * NY) == mz, 0, 1), lax.rem(shard // NX, NY)]
        return remote(block, near_ref.at[o + 2, g // SPLIT, :, :, lanes(g)],
                      w_send.at[g, n], w_recv.at[g, n], to=to)

    def x_copy(g, way, i):
        return remote(out_buf.at[g, way, i], in_buf.at[g, way, i], x_send.at[g, way, i],
                      x_recv.at[g, way, i], to=x_peer[1] if way == 0 else x_peer[3])

    def x_phase(g, i):
        for way in range(2):
            dest = mx if i == 3 else wrap(mx + ((3 - i) if way == 0 else (1 + i)), NX)
            if i > 0:
                x_copy(g, way, i - 1).wait_recv()

            def fill(j, carry):
                slot = j + way * HALF
                block_id = ids_smem[dest, 0, slot]
                shard = block_id // PER
                picked = col[g][jnp.where(shard // (NX * NY) == mz, 0, 1),
                                lax.rem(shard // NX, NY), lax.rem(block_id, PER)]
                if i > 0:
                    mine = lax.rem(shard, NX) == mx
                    picked = lax.select(mine, picked, in_buf[g, way, i - 1, j])
                if i == 3:
                    sel_ref[g // SPLIT, slot, :, lanes(g)] = picked
                else:
                    out_buf[g, way, i, j] = picked
                return carry

            lax.fori_loop(0, HALF, fill, 0)
            if i < 3:
                begin(x_copy(g, way, i))

    y_phase(0, 0, 0)
    for copy in z_copies:
        begin(copy)
    own_ids.wait()
    for i in (1, 2, 3):
        begin(remote(ids_ref, ids_all.at[mx], id_send.at[i - 1], id_recv.at[i - 1], to=x_peer[i]))
    keep_own = []
    for g in range(GROUPS):
        own[g].wait()
        copy = pltpu.make_async_copy(col[g].at[0, my], near_ref.at[2, g // SPLIT, :, :, lanes(g)],
                                     keep_sem.at[g])
        copy.start()
        keep_own.append(copy)

    first = {(zz, g): FIRST * (2 * g + zz) for g in range(GROUPS) for zz in range(2)}
    w_at = {first[1, g] + 1: g for g in range(GROUPS)}
    x_at = {}
    for g in range(GROUPS):
        for i in range(4):
            x_at.setdefault(first[1, g] + X_LAG + X_GAP * i, []).append((g, i))
    for tick in range(1, max(x_at) + 1):
        for (zz, g), start in first.items():
            if 0 <= tick - start <= 4:
                y_phase(zz, g, tick - start)
        if tick in w_at:
            for n in range(4):
                begin(w_copy(w_at[tick], n))
        if tick == first[1, 0] + 4:
            for i in (1, 2, 3):
                remote(ids_ref, ids_all.at[wrap(mx - i, NX)], id_send.at[i - 1],
                       id_recv.at[i - 1], to=x_peer[i]).wait_recv()
            to_smem = pltpu.make_async_copy(ids_all, ids_smem, smem_sem.at[1])
            to_smem.start()
            to_smem.wait()
        for g, i in x_at.get(tick, ()):
            x_phase(g, i)

    for copy in keep_own:
        copy.wait()
    for g in range(GROUPS):
        for n in range(4):
            w_copy(g, n).wait_recv()
    for copy in sends:
        copy.wait_send()


def exchange(ids, keys, values):
    width = keys.shape[-1]
    dma = pltpu.SemaphoreType.DMA
    hbm = pl.BlockSpec(memory_space=pl.ANY)
    vmem = pl.BlockSpec(memory_space=pltpu.VMEM)
    return pl.pallas_call(
        exchange_kernel,
        out_shape=(jax.ShapeDtypeStruct((5, 2, PER, BLK, width), jnp.bfloat16),
                   jax.ShapeDtypeStruct((2, SLOTS, BLK, width), jnp.bfloat16)),
        in_specs=[vmem, hbm, hbm],
        out_specs=(hbm, vmem),
        scratch_shapes=[pltpu.VMEM((2, NY, PER, BLK, LANES), jnp.bfloat16)] * GROUPS + [
            pltpu.VMEM((GROUPS, 2, 3, HALF, BLK, LANES), jnp.bfloat16),
            pltpu.VMEM((GROUPS, 2, 3, HALF, BLK, LANES), jnp.bfloat16),
            pltpu.VMEM((NX, 8, 128), jnp.int32),
            pltpu.SMEM((NX, 8, 128), jnp.int32),
            dma((GROUPS,)), dma((GROUPS,)), dma((3,)), dma((3,)), dma((GROUPS,)), dma((GROUPS,)),
            dma((GROUPS, 4)), dma((GROUPS, 4)),
            dma((2, GROUPS, 2, 4)), dma((2, GROUPS, 2, 4)),
            dma((GROUPS, 2, 3)), dma((GROUPS, 2, 3)), dma((2,)),
        ],
        compiler_params=pltpu.CompilerParams(
            collective_id=0, has_side_effects=True, vmem_limit_bytes=48 << 20),
        name="exchange",
    )(ids, keys, values)


def attend_kernel(win_ref, q_ref, near_ref, sel_ref, out_ref, square_ref, key_buf, value_buf):
    b = pl.program_id(0)
    s = lax.axis_index("seq")
    for j in range(WIN):
        block_id = win_ref[b, j]
        o = lax.rem(block_id // PER - s + 2 + SHARDS, SHARDS)
        w = lax.rem(block_id, PER)
        rows = pl.ds(j * BLK, BLK)
        key_buf[rows, :] = near_ref[o, 0, w]
        value_buf[rows, :] = near_ref[o, 1, w]
    for r in range(5):
        slot = b * 3 + r if r < 3 else RANDS + r - 3
        rows = pl.ds((WIN + r) * BLK, BLK)
        key_buf[rows, :] = sel_ref[0, slot]
        value_buf[rows, :] = sel_ref[1, slot]
    squares = jnp.zeros(square_ref.shape[1:], jnp.float32)
    for h in range(q_ref.shape[-1] // HD):
        lanes = slice(h * HD, (h + 1) * HD)
        scores = lax.dot_general(q_ref[0, :, lanes], key_buf[:, lanes], (((1,), (1,)), ((), ())),
                                 preferred_element_type=jnp.float32)
        peak = jnp.max(scores, axis=-1, keepdims=True)
        lifted = jnp.exp((scores - peak) * HD ** -0.5)
        total = jnp.sum(lifted, axis=-1, keepdims=True)
        part = jnp.dot(lifted.astype(jnp.bfloat16), value_buf[:, lanes],
                       preferred_element_type=jnp.float32)
        attended = part / total
        squares += attended * attended
        out_ref[0, :, lanes] = attended
    square_ref[0] = squares


def attend(window, queries, near, sel):
    width = queries.shape[-1]
    keys_total = (WIN + 5) * BLK
    whole = lambda shape: pl.BlockSpec(shape, lambda b, *_: (0,) * len(shape),
                                       pipeline_mode=pl.Buffered(1))
    return pl.pallas_call(
        attend_kernel,
        out_shape=(jax.ShapeDtypeStruct((PER, BLK, width), jnp.float32),
                   jax.ShapeDtypeStruct((PER, BLK, HD), jnp.float32)),
        grid_spec=pltpu.PrefetchScalarGridSpec(
            num_scalar_prefetch=1, grid=(PER,),
            in_specs=[pl.BlockSpec((1, BLK, width), lambda b, *_: (b, 0, 0)),
                      whole(near.shape), whole(sel.shape)],
            out_specs=(pl.BlockSpec((1, BLK, width), lambda b, *_: (b, 0, 0)),
                       pl.BlockSpec((1, BLK, HD), lambda b, *_: (b, 0, 0))),
            scratch_shapes=[pltpu.VMEM((keys_total, width), jnp.bfloat16),
                            pltpu.VMEM((keys_total, width), jnp.bfloat16)]),
        compiler_params=pltpu.CompilerParams(vmem_limit_bytes=48 << 20),
        name="attend",
    )(window, queries, near, sel)


def norm_kernel(heads, attended_ref, square_ref, gain_ref, out_ref, sums, send_sem, recv_sem):
    me = lax.axis_index("head")
    peers = [lax.rem(me + i, heads) for i in range(1, heads)]
    await_peers = greet("head", peers)
    sums[me] = lax.dot_general(
        jnp.ones((8, HD), jnp.float32), square_ref[...], (((1,), (1,)), ((), ())),
        precision=lax.Precision.HIGHEST, preferred_element_type=jnp.float32)
    await_peers()
    copies = [remote_copy(sums.at[me], sums.at[me], send_sem.at[i], recv_sem.at[i], "head", peer)
              for i, peer in enumerate(peers)]
    for copy in copies:
        copy.start()
    for i in range(heads - 1):
        source = lax.rem(me + heads - 1 - i, heads)
        remote_copy(sums.at[source], sums.at[source], send_sem.at[i], recv_sem.at[i], "head",
                    peers[i]).wait_recv()
    total = sums[0]
    for i in range(1, heads):
        total += sums[i]
    inverse = jnp.transpose(lax.rsqrt(total / D + 1e-06))[:, :1]
    out_ref[...] = (attended_ref[...] * inverse * gain_ref[...]).astype(out_ref.dtype)
    for copy in copies:
        copy.wait_send()


def norm(attended, squares, gain):
    heads = lax.axis_size("head")
    dma = pltpu.SemaphoreType.DMA((heads - 1,))
    vmem = pl.BlockSpec(memory_space=pltpu.VMEM)
    return pl.pallas_call(
        partial(norm_kernel, heads),
        out_shape=jax.ShapeDtypeStruct(attended.shape, jnp.bfloat16),
        in_specs=[vmem] * 3,
        out_specs=vmem,
        scratch_shapes=[pltpu.VMEM((heads, 8, attended.shape[0]), jnp.float32), dma, dma],
        compiler_params=pltpu.CompilerParams(collective_id=1, has_side_effects=True),
        name="norm",
    )(attended, squares, gain)


def body(queries, key_rows, value_rows, window, random_blocks, global_blocks, norm_gain):
    width = queries.shape[1]
    blocks = lambda rows: rows.reshape(PER, BLK, width)
    ids = jnp.concatenate([random_blocks.reshape(-1), global_blocks])
    ids = jnp.broadcast_to(jnp.pad(ids, (0, 128 - SLOTS))[None, :], (8, 128))
    near, sel = exchange(ids, blocks(key_rows), blocks(value_rows))
    attended, squares = attend(window, blocks(queries), near, sel)
    return norm(attended.reshape(-1, width), squares.reshape(-1, HD), norm_gain[None, :])


def solution(mesh):
    placed = (
        P("seq", "head"),
        P("seq", "head"),
        P("seq", "head"),
        P("seq", None),
        P("seq", None),
        P(),
        P("head"),
    )
    return jax.shard_map(
        body, mesh=mesh, in_specs=placed, out_specs=P("seq", "head"), check_vma=False
    )
```

```python
from functools import partial

import jax
import jax.numpy as jnp
from jax import lax
from jax.experimental import pallas as pl
from jax.experimental.pallas import tpu as pltpu
from jax.sharding import PartitionSpec as P

HD = 128
D = 4096
BLK = 64
NX, NY, NZ = 4, 8, 2
SHARDS = NX * NY * NZ
PER = 4
RANDS = 12
SLOTS = 14
HALF = 7
WIN = 12
PARTS = ((0, 0, 128), (0, 128, 256), (0, 384, 128), (1, 0, 256), (1, 256, 256))
GROUPS = len(PARTS)
PERIOD, EARLY, NEAR_AT, X_GAP = 3, 2, 1, 2
MESH = pl.DeviceIdType.MESH


def remote_copy(src, dst, send, recv, axis, to):
    return pltpu.make_async_remote_copy(
        src_ref=src, dst_ref=dst, send_sem=send, recv_sem=recv,
        device_id={axis: to}, device_id_type=MESH)


def greet(axis, peers):
    barrier = pltpu.get_barrier_semaphore()
    for peer in peers:
        pl.semaphore_signal(barrier, inc=1, device_id={axis: peer}, device_id_type=MESH)
    return lambda: pl.semaphore_wait(barrier, len(peers))


def exchange_kernel(ids_ref, k_ref, v_ref, near_ref, sel_ref, *scratch):
    col = scratch[:GROUPS]
    out_buf, in_buf = scratch[GROUPS:2 * GROUPS], scratch[2 * GROUPS:3 * GROUPS]
    (ids_all, ids_smem, own_sem, keep_sem, id_send, id_recv, z_send, z_recv,
     w_send, w_recv, y_send, y_recv, x_send, x_recv, smem_sem) = scratch[3 * GROUPS:]
    s = lax.axis_index("seq")
    mx = lax.rem(s, NX)
    my = lax.rem(s // NX, NY)
    mz = s // (NX * NY)
    remote = partial(remote_copy, axis="seq")

    def lanes(g):
        return pl.ds(PARTS[g][1], PARTS[g][2])

    own_kv = [(k_ref, v_ref)[PARTS[g][0]].at[:, :, lanes(g)] for g in range(GROUPS)]

    def at(z, y, x):
        return z * (NX * NY) + y * NX + x

    def wrap(value, size):
        return lax.rem(value + 2 * size, size)

    z_peer = at(1 - mz, my, mx)
    y_peer = (at(mz, wrap(my + 1, NY), mx), at(mz, wrap(my - 1, NY), mx))
    x_peer = [at(mz, my, wrap(mx + i, NX)) for i in range(NX)]

    await_peers = greet("seq", [z_peer, *y_peer, *x_peer[1:]])
    own = [pltpu.make_async_copy(own_kv[g], col[g].at[0, my], own_sem.at[g]) for g in range(GROUPS)]
    own_ids = pltpu.make_async_copy(ids_ref, ids_all.at[mx], smem_sem.at[0])
    for copy in own:
        copy.start()
    own_ids.start()
    await_peers()

    sends = []

    def begin(copy):
        copy.start()
        sends.append(copy)

    def y_copy(zz, g, way, t, y_src):
        part = pl.ds(0, PER) if t < 4 else pl.ds(2 * way, 2)
        block = col[g].at[zz, y_src, part]
        source = own_kv[g] if t == 1 and zz == 0 else block
        return remote(source, block, y_send.at[zz, g, way, t - 1],
                      y_recv.at[zz, g, way, t - 1], to=y_peer[way])

    def y_start(zz, g, t):
        for way, sign in ((0, 1), (1, -1)):
            begin(y_copy(zz, g, way, t, wrap(my - sign * (t - 1), NY)))

    def y_wait(zz, g, t):
        for way, sign in ((0, 1), (1, -1)):
            y_copy(zz, g, way, t, wrap(my - sign * t, NY)).wait_recv()

    z_copies = [remote(own_kv[g], col[g].at[1, my], z_send.at[g], z_recv.at[g], to=z_peer)
                for g in range(GROUPS)]

    def y_phase(zz, g, t):
        y_wait(zz, g, t)
        if t < 4:
            y_start(zz, g, t + 1)

    def w_copy(g, n):
        away, o = ((1, -1), (-1, 1), (2, 2), (2, -2))[n]
        to = x_peer[away % NX]
        shard = wrap(to + o, SHARDS)
        block = col[g].at[jnp.where(shard // (NX * NY) == mz, 0, 1), lax.rem(shard // NX, NY)]
        return remote(block, near_ref.at[o + 2, PARTS[g][0], :, :, lanes(g)],
                      w_send.at[g, n], w_recv.at[g, n], to=to)

    def x_copy(g, way, i):
        return remote(out_buf[g].at[way, i], in_buf[g].at[way, i], x_send.at[g, way, i],
                      x_recv.at[g, way, i], to=x_peer[1] if way == 0 else x_peer[3])

    def x_phase(g, i):
        for way in range(2):
            dest = mx if i == 3 else wrap(mx + ((3 - i) if way == 0 else (1 + i)), NX)
            if i > 0:
                x_copy(g, way, i - 1).wait_recv()

            def fill(j, carry):
                slot = j + way * HALF
                block_id = ids_smem[dest, 0, slot]
                shard = block_id // PER
                picked = col[g][jnp.where(shard // (NX * NY) == mz, 0, 1),
                                lax.rem(shard // NX, NY), lax.rem(block_id, PER)]
                if i > 0:
                    mine = lax.rem(shard, NX) == mx
                    picked = lax.select(mine, picked, in_buf[g][way, i - 1, j])
                if i == 3:
                    sel_ref[PARTS[g][0], slot, :, lanes(g)] = picked
                else:
                    out_buf[g][way, i, j] = picked
                return carry

            lax.fori_loop(0, HALF, fill, 0)
            if i < 3:
                begin(x_copy(g, way, i))

    for g in range(GROUPS):
        if g * PERIOD <= EARLY:
            y_start(0, g, 1)
        begin(z_copies[g])
    own_ids.wait()
    for i in (1, 2, 3):
        begin(remote(ids_ref, ids_all.at[mx], id_send.at[i - 1], id_recv.at[i - 1], to=x_peer[i]))
    keep_own = []
    for g in range(GROUPS):
        own[g].wait()
        copy = pltpu.make_async_copy(col[g].at[0, my], near_ref.at[2, PARTS[g][0], :, :, lanes(g)],
                                     keep_sem.at[g])
        copy.start()
        keep_own.append(copy)

    x_at = {}
    for g in range(GROUPS):
        for i in range(4):
            x_at.setdefault(PERIOD * g + 4 + X_GAP * i, []).append((g, i))
    for tick in range(max(x_at) + 1):
        for g in range(GROUPS):
            start = max(0, PERIOD * g - EARLY)
            if tick == start:
                if start > 0:
                    y_start(0, g, 1)
                z_copies[g].wait_recv()
                y_start(1, g, 1)
        for g in range(GROUPS):
            t = tick - PERIOD * g
            if 1 <= t <= 4:
                for zz in range(2):
                    y_phase(zz, g, t)
            if t == NEAR_AT:
                for n in range(4):
                    begin(w_copy(g, n))
        if tick == 4:
            for i in (1, 2, 3):
                remote(ids_ref, ids_all.at[wrap(mx - i, NX)], id_send.at[i - 1],
                       id_recv.at[i - 1], to=x_peer[i]).wait_recv()
            to_smem = pltpu.make_async_copy(ids_all, ids_smem, smem_sem.at[1])
            to_smem.start()
            to_smem.wait()
        for g, i in x_at.get(tick, ()):
            x_phase(g, i)

    for copy in keep_own:
        copy.wait()
    for g in range(GROUPS):
        for n in range(4):
            w_copy(g, n).wait_recv()
    for copy in sends:
        copy.wait_send()


def exchange(ids, keys, values):
    width = keys.shape[-1]
    dma = pltpu.SemaphoreType.DMA
    hbm = pl.BlockSpec(memory_space=pl.ANY)
    vmem = pl.BlockSpec(memory_space=pltpu.VMEM)
    return pl.pallas_call(
        exchange_kernel,
        out_shape=(jax.ShapeDtypeStruct((5, 2, PER, BLK, width), jnp.bfloat16),
                   jax.ShapeDtypeStruct((2, SLOTS, BLK, width), jnp.bfloat16)),
        in_specs=[vmem, hbm, hbm],
        out_specs=(hbm, vmem),
        scratch_shapes=[
            *[pltpu.VMEM((2, NY, PER, BLK, part[2]), jnp.bfloat16) for part in PARTS],
            *[pltpu.VMEM((2, 3, HALF, BLK, part[2]), jnp.bfloat16) for part in PARTS * 2],
            pltpu.VMEM((NX, 8, 128), jnp.int32),
            pltpu.SMEM((NX, 8, 128), jnp.int32),
            dma((GROUPS,)), dma((GROUPS,)), dma((3,)), dma((3,)), dma((GROUPS,)), dma((GROUPS,)),
            dma((GROUPS, 4)), dma((GROUPS, 4)),
            dma((2, GROUPS, 2, 4)), dma((2, GROUPS, 2, 4)),
            dma((GROUPS, 2, 3)), dma((GROUPS, 2, 3)), dma((2,)),
        ],
        compiler_params=pltpu.CompilerParams(
            collective_id=0, has_side_effects=True, vmem_limit_bytes=48 << 20),
        name="exchange",
    )(ids, keys, values)


def attend_kernel(win_ref, q_ref, near_ref, sel_ref, out_ref, square_ref, key_buf, value_buf):
    b = pl.program_id(0)
    s = lax.axis_index("seq")
    for j in range(WIN):
        block_id = win_ref[b, j]
        o = lax.rem(block_id // PER - s + 2 + SHARDS, SHARDS)
        w = lax.rem(block_id, PER)
        rows = pl.ds(j * BLK, BLK)
        key_buf[rows, :] = near_ref[o, 0, w]
        value_buf[rows, :] = near_ref[o, 1, w]
    for r in range(5):
        slot = b * 3 + r if r < 3 else RANDS + r - 3
        rows = pl.ds((WIN + r) * BLK, BLK)
        key_buf[rows, :] = sel_ref[0, slot]
        value_buf[rows, :] = sel_ref[1, slot]
    squares = jnp.zeros(square_ref.shape[1:], jnp.float32)
    for h in range(q_ref.shape[-1] // HD):
        lanes = slice(h * HD, (h + 1) * HD)
        scores = lax.dot_general(q_ref[0, :, lanes], key_buf[:, lanes], (((1,), (1,)), ((), ())),
                                 preferred_element_type=jnp.float32)
        peak = jnp.max(scores, axis=-1, keepdims=True)
        lifted = jnp.exp((scores - peak) * HD ** -0.5)
        total = jnp.sum(lifted, axis=-1, keepdims=True)
        part = jnp.dot(lifted.astype(jnp.bfloat16), value_buf[:, lanes],
                       preferred_element_type=jnp.float32)
        attended = part / total
        squares += attended * attended
        out_ref[0, :, lanes] = attended
    square_ref[0] = squares


def attend(window, queries, near, sel):
    width = queries.shape[-1]
    keys_total = (WIN + 5) * BLK
    whole = lambda shape: pl.BlockSpec(shape, lambda b, *_: (0,) * len(shape),
                                       pipeline_mode=pl.Buffered(1))
    return pl.pallas_call(
        attend_kernel,
        out_shape=(jax.ShapeDtypeStruct((PER, BLK, width), jnp.float32),
                   jax.ShapeDtypeStruct((PER, BLK, HD), jnp.float32)),
        grid_spec=pltpu.PrefetchScalarGridSpec(
            num_scalar_prefetch=1, grid=(PER,),
            in_specs=[pl.BlockSpec((1, BLK, width), lambda b, *_: (b, 0, 0)),
                      whole(near.shape), whole(sel.shape)],
            out_specs=(pl.BlockSpec((1, BLK, width), lambda b, *_: (b, 0, 0)),
                       pl.BlockSpec((1, BLK, HD), lambda b, *_: (b, 0, 0))),
            scratch_shapes=[pltpu.VMEM((keys_total, width), jnp.bfloat16),
                            pltpu.VMEM((keys_total, width), jnp.bfloat16)]),
        compiler_params=pltpu.CompilerParams(vmem_limit_bytes=48 << 20),
        name="attend",
    )(window, queries, near, sel)


def norm_kernel(heads, attended_ref, square_ref, gain_ref, out_ref, sums, send_sem, recv_sem):
    me = lax.axis_index("head")
    peers = [lax.rem(me + i, heads) for i in range(1, heads)]
    await_peers = greet("head", peers)
    sums[me] = lax.dot_general(
        jnp.ones((8, HD), jnp.float32), square_ref[...], (((1,), (1,)), ((), ())),
        precision=lax.Precision.HIGHEST, preferred_element_type=jnp.float32)
    await_peers()
    copies = [remote_copy(sums.at[me], sums.at[me], send_sem.at[i], recv_sem.at[i], "head", peer)
              for i, peer in enumerate(peers)]
    for copy in copies:
        copy.start()
    for i in range(heads - 1):
        source = lax.rem(me + heads - 1 - i, heads)
        remote_copy(sums.at[source], sums.at[source], send_sem.at[i], recv_sem.at[i], "head",
                    peers[i]).wait_recv()
    total = sums[0]
    for i in range(1, heads):
        total += sums[i]
    inverse = jnp.transpose(lax.rsqrt(total / D + 1e-06))[:, :1]
    out_ref[...] = (attended_ref[...] * inverse * gain_ref[...]).astype(out_ref.dtype)
    for copy in copies:
        copy.wait_send()


def norm(attended, squares, gain):
    heads = lax.axis_size("head")
    dma = pltpu.SemaphoreType.DMA((heads - 1,))
    vmem = pl.BlockSpec(memory_space=pltpu.VMEM)
    return pl.pallas_call(
        partial(norm_kernel, heads),
        out_shape=jax.ShapeDtypeStruct(attended.shape, jnp.bfloat16),
        in_specs=[vmem] * 3,
        out_specs=vmem,
        scratch_shapes=[pltpu.VMEM((heads, 8, attended.shape[0]), jnp.float32), dma, dma],
        compiler_params=pltpu.CompilerParams(collective_id=1, has_side_effects=True),
        name="norm",
    )(attended, squares, gain)


def body(queries, key_rows, value_rows, window, random_blocks, global_blocks, norm_gain):
    width = queries.shape[1]
    blocks = lambda rows: rows.reshape(PER, BLK, width)
    ids = jnp.concatenate([random_blocks.reshape(-1), global_blocks])
    ids = jnp.broadcast_to(jnp.pad(ids, (0, 128 - SLOTS))[None, :], (8, 128))
    near, sel = exchange(ids, blocks(key_rows), blocks(value_rows))
    attended, squares = attend(window, blocks(queries), near, sel)
    return norm(attended.reshape(-1, width), squares.reshape(-1, HD), norm_gain[None, :])


def solution(mesh):
    placed = (
        P("seq", "head"),
        P("seq", "head"),
        P("seq", "head"),
        P("seq", None),
        P("seq", None),
        P(),
        P("head"),
    )
    return jax.shard_map(
        body, mesh=mesh, in_specs=placed, out_specs=P("seq", "head"), check_vma=False
    )
```

```python
from functools import partial

import jax
import jax.numpy as jnp
from jax import lax
from jax.experimental import pallas as pl
from jax.experimental.pallas import tpu as pltpu
from jax.sharding import PartitionSpec as P

HD = 128
D = 4096
BLK = 64
NX, NY, NZ = 4, 8, 2
SHARDS = NX * NY * NZ
PER = 4
RANDS = 12
SLOTS = 14
HALF = 7
WIN = 12
PARTS = ((0, 0, 128), (0, 128, 256), (0, 384, 128), (1, 0, 256), (1, 256, 256))
GROUPS = len(PARTS)
PERIOD, EARLY, NEAR_AT, X_GAP = 3, 2, 1, 2
MESH = pl.DeviceIdType.MESH


def remote_copy(src, dst, send, recv, axis, to):
    return pltpu.make_async_remote_copy(
        src_ref=src, dst_ref=dst, send_sem=send, recv_sem=recv,
        device_id={axis: to}, device_id_type=MESH)


def greet(axis, peers):
    barrier = pltpu.get_barrier_semaphore()
    for peer in peers:
        pl.semaphore_signal(barrier, inc=1, device_id={axis: peer}, device_id_type=MESH)
    return lambda: pl.semaphore_wait(barrier, len(peers))


def exchange_kernel(ids_ref, k_ref, v_ref, near_ref, sel_ref, *scratch):
    col = scratch[:GROUPS]
    out_buf, in_buf = scratch[GROUPS:2 * GROUPS], scratch[2 * GROUPS:3 * GROUPS]
    (ids_all, ids_smem, own_sem, keep_sem, id_send, id_recv, z_send, z_recv,
     w_send, w_recv, y_send, y_recv, x_send, x_recv, smem_sem) = scratch[3 * GROUPS:]
    s = lax.axis_index("seq")
    mx = lax.rem(s, NX)
    my = lax.rem(s // NX, NY)
    mz = s // (NX * NY)
    remote = partial(remote_copy, axis="seq")

    def lanes(g):
        return pl.ds(PARTS[g][1], PARTS[g][2])

    own_kv = [(k_ref, v_ref)[PARTS[g][0]].at[:, :, lanes(g)] for g in range(GROUPS)]

    def at(z, y, x):
        return z * (NX * NY) + y * NX + x

    def wrap(value, size):
        return lax.rem(value + 2 * size, size)

    z_peer = at(1 - mz, my, mx)
    y_peer = (at(mz, wrap(my + 1, NY), mx), at(mz, wrap(my - 1, NY), mx))
    x_peer = [at(mz, my, wrap(mx + i, NX)) for i in range(NX)]

    await_peers = greet("seq", [z_peer, *y_peer, *x_peer[1:]])
    own = [pltpu.make_async_copy(own_kv[g], col[g].at[0, my], own_sem.at[g]) for g in range(GROUPS)]
    own_ids = pltpu.make_async_copy(ids_ref, ids_all.at[mx], smem_sem.at[0])
    for copy in own:
        copy.start()
    own_ids.start()
    await_peers()

    sends = []

    def begin(copy):
        copy.start()
        sends.append(copy)

    def y_copy(zz, g, way, t, y_src):
        part = pl.ds(0, PER) if t < 4 else pl.ds(2 * way, 2)
        block = col[g].at[zz, y_src, part]
        source = own_kv[g] if t == 1 and zz == 0 else block
        return remote(source, block, y_send.at[zz, g, way, t - 1],
                      y_recv.at[zz, g, way, t - 1], to=y_peer[way])

    def y_start(zz, g, t):
        for way, sign in ((0, 1), (1, -1)):
            begin(y_copy(zz, g, way, t, wrap(my - sign * (t - 1), NY)))

    def y_wait(zz, g, t):
        for way, sign in ((0, 1), (1, -1)):
            y_copy(zz, g, way, t, wrap(my - sign * t, NY)).wait_recv()

    z_copies = [remote(own_kv[g], col[g].at[1, my], z_send.at[g], z_recv.at[g], to=z_peer)
                for g in range(GROUPS)]

    def y_phase(zz, g, t):
        y_wait(zz, g, t)
        if t < 4:
            y_start(zz, g, t + 1)

    def w_copy(g, n):
        away, o = ((1, -1), (-1, 1), (2, 2), (2, -2))[n]
        to = x_peer[away % NX]
        shard = wrap(to + o, SHARDS)
        block = col[g].at[jnp.where(shard // (NX * NY) == mz, 0, 1), lax.rem(shard // NX, NY)]
        return remote(block, near_ref.at[o + 2, PARTS[g][0], :, :, lanes(g)],
                      w_send.at[g, n], w_recv.at[g, n], to=to)

    def x_copy(g, way, i):
        return remote(out_buf[g].at[way, i], in_buf[g].at[way, i], x_send.at[g, way, i],
                      x_recv.at[g, way, i], to=x_peer[1] if way == 0 else x_peer[3])

    def x_phase(g, i):
        for way in range(2):
            dest = mx if i == 3 else wrap(mx + ((3 - i) if way == 0 else (1 + i)), NX)
            if i > 0:
                x_copy(g, way, i - 1).wait_recv()

            def fill(j, carry):
                slot = j + way * HALF
                block_id = ids_smem[dest, 0, slot]
                shard = block_id // PER
                picked = col[g][jnp.where(shard // (NX * NY) == mz, 0, 1),
                                lax.rem(shard // NX, NY), lax.rem(block_id, PER)]
                if i > 0:
                    mine = lax.rem(shard, NX) == mx
                    picked = lax.select(mine, picked, in_buf[g][way, i - 1, j])
                if i == 3:
                    sel_ref[PARTS[g][0], slot, :, lanes(g)] = picked
                else:
                    out_buf[g][way, i, j] = picked
                return carry

            lax.fori_loop(0, HALF, fill, 0)
            if i < 3:
                begin(x_copy(g, way, i))

    for g in range(GROUPS):
        if g * PERIOD <= EARLY:
            y_start(0, g, 1)
        begin(z_copies[g])
    own_ids.wait()
    for i in (1, 2, 3):
        begin(remote(ids_ref, ids_all.at[mx], id_send.at[i - 1], id_recv.at[i - 1], to=x_peer[i]))
    keep_own = []
    for g in range(GROUPS):
        own[g].wait()
        copy = pltpu.make_async_copy(col[g].at[0, my], near_ref.at[2, PARTS[g][0], :, :, lanes(g)],
                                     keep_sem.at[g])
        copy.start()
        keep_own.append(copy)

    x_at = {}
    for g in range(GROUPS):
        for i in range(4):
            x_at.setdefault(PERIOD * g + 4 + X_GAP * i, []).append((g, i))
    for tick in range(max(x_at) + 1):
        for g in range(GROUPS):
            start = max(0, PERIOD * g - EARLY)
            if tick == start:
                if start > 0:
                    y_start(0, g, 1)
                z_copies[g].wait_recv()
                y_start(1, g, 1)
        for g in range(GROUPS):
            t = tick - PERIOD * g
            if 1 <= t <= 4:
                for zz in range(2):
                    y_phase(zz, g, t)
            if t == NEAR_AT:
                for n in range(4):
                    begin(w_copy(g, n))
        if tick == 4:
            for i in (1, 2, 3):
                remote(ids_ref, ids_all.at[wrap(mx - i, NX)], id_send.at[i - 1],
                       id_recv.at[i - 1], to=x_peer[i]).wait_recv()
            to_smem = pltpu.make_async_copy(ids_all, ids_smem, smem_sem.at[1])
            to_smem.start()
            to_smem.wait()
        for g, i in x_at.get(tick, ()):
            x_phase(g, i)

    for copy in keep_own:
        copy.wait()
    for g in range(GROUPS):
        for n in range(4):
            w_copy(g, n).wait_recv()
    for copy in sends:
        copy.wait_send()


def exchange(ids, keys, values):
    width = keys.shape[-1]
    dma = pltpu.SemaphoreType.DMA
    hbm = pl.BlockSpec(memory_space=pl.ANY)
    vmem = pl.BlockSpec(memory_space=pltpu.VMEM)
    return pl.pallas_call(
        exchange_kernel,
        out_shape=(jax.ShapeDtypeStruct((5, 2, PER, BLK, width), jnp.bfloat16),
                   jax.ShapeDtypeStruct((2, SLOTS, BLK, width), jnp.bfloat16)),
        in_specs=[vmem, hbm, hbm],
        out_specs=(hbm, vmem),
        scratch_shapes=[
            *[pltpu.VMEM((2, NY, PER, BLK, part[2]), jnp.bfloat16) for part in PARTS],
            *[pltpu.VMEM((2, 3, HALF, BLK, part[2]), jnp.bfloat16) for part in PARTS * 2],
            pltpu.VMEM((NX, 8, 128), jnp.int32),
            pltpu.SMEM((NX, 8, 128), jnp.int32),
            dma((GROUPS,)), dma((GROUPS,)), dma((3,)), dma((3,)), dma((GROUPS,)), dma((GROUPS,)),
            dma((GROUPS, 4)), dma((GROUPS, 4)),
            dma((2, GROUPS, 2, 4)), dma((2, GROUPS, 2, 4)),
            dma((GROUPS, 2, 3)), dma((GROUPS, 2, 3)), dma((2,)),
        ],
        compiler_params=pltpu.CompilerParams(
            collective_id=0, has_side_effects=True, vmem_limit_bytes=48 << 20),
        name="exchange",
    )(ids, keys, values)


def attend_kernel(heads, win_ref, q_ref, near_ref, sel_ref, gain_ref, out_ref,
                  key_buf, value_buf, attended_buf, square_buf, sums, send_sem, recv_sem):
    me = lax.axis_index("head")
    s = lax.axis_index("seq")
    peers = [lax.rem(me + i, heads) for i in range(1, heads)]
    await_peers = greet("head", peers)

    def one_block(b, carry):
        for j in range(WIN):
            block_id = win_ref[b, j]
            o = jnp.minimum(lax.rem(block_id // PER - s + 2 + SHARDS, SHARDS), 4)
            w = lax.rem(block_id, PER)
            rows = pl.ds(j * BLK, BLK)
            key_buf[rows, :] = near_ref[o, 0, w]
            value_buf[rows, :] = near_ref[o, 1, w]
        for r in range(5):
            slot = b * 3 + r if r < 3 else RANDS + r - 3
            rows = pl.ds((WIN + r) * BLK, BLK)
            key_buf[rows, :] = sel_ref[0, slot]
            value_buf[rows, :] = sel_ref[1, slot]
        squares = jnp.zeros((BLK, HD), jnp.float32)
        for h in range(q_ref.shape[-1] // HD):
            lanes = slice(h * HD, (h + 1) * HD)
            scores = lax.dot_general(q_ref[b, :, lanes], key_buf[:, lanes], (((1,), (1,)), ((), ())),
                                     preferred_element_type=jnp.float32)
            peak = jnp.max(scores, axis=-1, keepdims=True)
            lifted = jnp.exp((scores - peak) * HD ** -0.5)
            total = jnp.sum(lifted, axis=-1, keepdims=True)
            part = jnp.dot(lifted.astype(jnp.bfloat16), value_buf[:, lanes],
                           preferred_element_type=jnp.float32)
            attended = part / total
            squares += attended * attended
            attended_buf[b, :, lanes] = attended
        square_buf[b] = squares
        return carry

    lax.fori_loop(0, PER, one_block, 0)
    sums[me] = lax.dot_general(
        jnp.ones((8, HD), jnp.float32), square_buf[...].reshape(PER * BLK, HD),
        (((1,), (1,)), ((), ())),
        precision=lax.Precision.HIGHEST, preferred_element_type=jnp.float32)
    await_peers()
    copies = [remote_copy(sums.at[me], sums.at[me], send_sem.at[i], recv_sem.at[i], "head", peer)
              for i, peer in enumerate(peers)]
    for copy in copies:
        copy.start()
    for i in range(heads - 1):
        source = lax.rem(me + heads - 1 - i, heads)
        remote_copy(sums.at[source], sums.at[source], send_sem.at[i], recv_sem.at[i], "head",
                    peers[i]).wait_recv()
    total = sums[0]
    for i in range(1, heads):
        total += sums[i]
    inverse = jnp.transpose(lax.rsqrt(total / D + 1e-06))[:, :1]
    for b in range(PER):
        rows = slice(b * BLK, (b + 1) * BLK)
        out_ref[rows, :] = (attended_buf[b] * inverse[rows] * gain_ref[...]).astype(out_ref.dtype)
    for copy in copies:
        copy.wait_send()


def attend(window, queries, near, sel, gain):
    width = queries.shape[-1]
    heads = lax.axis_size("head")
    keys_total = (WIN + 5) * BLK
    dma = pltpu.SemaphoreType.DMA((heads - 1,))
    vmem = pl.BlockSpec(memory_space=pltpu.VMEM)
    return pl.pallas_call(
        partial(attend_kernel, heads),
        out_shape=jax.ShapeDtypeStruct((PER * BLK, width), jnp.bfloat16),
        in_specs=[pl.BlockSpec(memory_space=pltpu.SMEM)] + [vmem] * 4,
        out_specs=vmem,
        scratch_shapes=[
            pltpu.VMEM((keys_total, width), jnp.bfloat16),
            pltpu.VMEM((keys_total, width), jnp.bfloat16),
            pltpu.VMEM((PER, BLK, width), jnp.float32),
            pltpu.VMEM((PER, BLK, HD), jnp.float32),
            pltpu.VMEM((heads, 8, PER * BLK), jnp.float32), dma, dma],
        compiler_params=pltpu.CompilerParams(
            collective_id=1, has_side_effects=True, vmem_limit_bytes=48 << 20),
        name="attend",
    )(window, queries, near, sel, gain)


def body(queries, key_rows, value_rows, window, random_blocks, global_blocks, norm_gain):
    width = queries.shape[1]
    blocks = lambda rows: rows.reshape(PER, BLK, width)
    ids = jnp.concatenate([random_blocks.reshape(-1), global_blocks])
    ids = jnp.broadcast_to(jnp.pad(ids, (0, 128 - SLOTS))[None, :], (8, 128))
    near, sel = exchange(ids, blocks(key_rows), blocks(value_rows))
    return attend(window, blocks(queries), near, sel, norm_gain[None, :])


def solution(mesh):
    placed = (
        P("seq", "head"),
        P("seq", "head"),
        P("seq", "head"),
        P("seq", None),
        P("seq", None),
        P(),
        P("head"),
    )
    return jax.shard_map(
        body, mesh=mesh, in_specs=placed, out_specs=P("seq", "head"), check_vma=False
    )
```

```python
from functools import partial

import jax
import jax.numpy as jnp
from jax import lax
from jax.experimental import pallas as pl
from jax.experimental.pallas import tpu as pltpu
from jax.sharding import PartitionSpec as P

HD = 128
D = 4096
BLK = 64
NX, NY, NZ = 4, 8, 2
SHARDS = NX * NY * NZ
PER = 4
RANDS = 12
SLOTS = 14
HALF = 7
WIN = 12
PARTS = ((0, 0, 128), (0, 128, 256), (0, 384, 128), (1, 0, 256), (1, 256, 256))
GROUPS = len(PARTS)
PERIOD, EARLY, NEAR_AT, X_GAP = 3, 2, 1, 2
MESH = pl.DeviceIdType.MESH


def remote_copy(src, dst, send, recv, axis, to):
    return pltpu.make_async_remote_copy(
        src_ref=src, dst_ref=dst, send_sem=send, recv_sem=recv,
        device_id={axis: to}, device_id_type=MESH)


def greet(seq_peers, head_peers):
    barrier = pltpu.get_barrier_semaphore()
    peers = [{"seq": peer} for peer in seq_peers] + [{"head": peer} for peer in head_peers]
    for peer in peers:
        pl.semaphore_signal(barrier, inc=1, device_id=peer, device_id_type=MESH)
    return lambda: pl.semaphore_wait(barrier, len(peers))


def exchange_kernel(heads, ids_ref, win_ref, k_ref, v_ref, q_ref, gain_ref, out_ref, *scratch):
    col = scratch[:GROUPS]
    out_buf, in_buf = scratch[GROUPS:2 * GROUPS], scratch[2 * GROUPS:3 * GROUPS]
    (ids_all, ids_smem, own_sem, keep_sem, id_send, id_recv, z_send, z_recv,
     w_send, w_recv, y_send, y_recv, x_send, x_recv, smem_sem, near_ref, sel_ref, key_buf, value_buf,
     attended_buf, square_buf, peak_buf, total_buf, sums, head_send, head_recv) = scratch[3 * GROUPS:]
    s = lax.axis_index("seq")
    me = lax.axis_index("head")
    head_peers = [lax.rem(me + i, heads) for i in range(1, heads)]
    mx = lax.rem(s, NX)
    my = lax.rem(s // NX, NY)
    mz = s // (NX * NY)
    remote = partial(remote_copy, axis="seq")

    def lanes(g):
        return pl.ds(PARTS[g][1], PARTS[g][2])

    own_kv = [(k_ref, v_ref)[PARTS[g][0]].at[:, :, lanes(g)] for g in range(GROUPS)]

    def at(z, y, x):
        return z * (NX * NY) + y * NX + x

    def wrap(value, size):
        return lax.rem(value + 2 * size, size)

    z_peer = at(1 - mz, my, mx)
    y_peer = (at(mz, wrap(my + 1, NY), mx), at(mz, wrap(my - 1, NY), mx))
    x_peer = [at(mz, my, wrap(mx + i, NX)) for i in range(NX)]

    await_peers = greet([z_peer, *y_peer, *x_peer[1:]], head_peers)
    own = [pltpu.make_async_copy(own_kv[g], col[g].at[0, my], own_sem.at[g]) for g in range(GROUPS)]
    own_ids = pltpu.make_async_copy(ids_ref, ids_all.at[mx], smem_sem.at[0])
    for copy in own:
        copy.start()
    own_ids.start()
    await_peers()

    sends = []

    def begin(copy):
        copy.start()
        sends.append(copy)

    def y_copy(zz, g, way, t, y_src):
        part = pl.ds(0, PER) if t < 4 else pl.ds(2 * way, 2)
        block = col[g].at[zz, y_src, part]
        source = own_kv[g] if t == 1 and zz == 0 else block
        return remote(source, block, y_send.at[zz, g, way, t - 1],
                      y_recv.at[zz, g, way, t - 1], to=y_peer[way])

    def y_start(zz, g, t):
        for way, sign in ((0, 1), (1, -1)):
            begin(y_copy(zz, g, way, t, wrap(my - sign * (t - 1), NY)))

    def y_wait(zz, g, t):
        for way, sign in ((0, 1), (1, -1)):
            y_copy(zz, g, way, t, wrap(my - sign * t, NY)).wait_recv()

    z_copies = [remote(own_kv[g], col[g].at[1, my], z_send.at[g], z_recv.at[g], to=z_peer)
                for g in range(GROUPS)]

    def y_phase(zz, g, t):
        y_wait(zz, g, t)
        if t < 4:
            y_start(zz, g, t + 1)

    def w_copy(g, n):
        away, o = ((1, -1), (-1, 1), (2, 2), (2, -2))[n]
        to = x_peer[away % NX]
        shard = wrap(to + o, SHARDS)
        block = col[g].at[jnp.where(shard // (NX * NY) == mz, 0, 1), lax.rem(shard // NX, NY)]
        return remote(block, near_ref.at[o + 2, PARTS[g][0], :, :, lanes(g)],
                      w_send.at[g, n], w_recv.at[g, n], to=to)

    def x_copy(g, way, i):
        return remote(out_buf[g].at[way, i], in_buf[g].at[way, i], x_send.at[g, way, i],
                      x_recv.at[g, way, i], to=x_peer[1] if way == 0 else x_peer[3])

    def x_phase(g, i):
        for way in range(2):
            dest = mx if i == 3 else wrap(mx + ((3 - i) if way == 0 else (1 + i)), NX)
            if i > 0:
                x_copy(g, way, i - 1).wait_recv()

            def fill(j, carry):
                slot = j + way * HALF
                block_id = ids_smem[dest, 0, slot]
                shard = block_id // PER
                picked = col[g][jnp.where(shard // (NX * NY) == mz, 0, 1),
                                lax.rem(shard // NX, NY), lax.rem(block_id, PER)]
                if i > 0:
                    mine = lax.rem(shard, NX) == mx
                    picked = lax.select(mine, picked, in_buf[g][way, i - 1, j])
                if i == 3:
                    sel_ref[PARTS[g][0], slot, :, lanes(g)] = picked
                else:
                    out_buf[g][way, i, j] = picked
                return carry

            lax.fori_loop(0, HALF, fill, 0)
            if i < 3:
                begin(x_copy(g, way, i))

    def softmax_part(b, count, h):
        lanes_h = slice(h * HD, (h + 1) * HD)
        scores = lax.dot_general(q_ref[b, :, lanes_h], key_buf[:count, lanes_h],
                                 (((1,), (1,)), ((), ())), preferred_element_type=jnp.float32)
        peak = jnp.max(scores, axis=-1, keepdims=True)
        lifted = jnp.exp((scores - peak) * HD ** -0.5)
        part = jnp.dot(lifted.astype(jnp.bfloat16), value_buf[:count, lanes_h],
                       preferred_element_type=jnp.float32)
        return peak, jnp.sum(lifted, axis=-1, keepdims=True), part

    def window_part(b, carry):
        for j in range(WIN):
            block_id = win_ref[b, j]
            o = jnp.minimum(lax.rem(block_id // PER - s + 2 + SHARDS, SHARDS), 4)
            w = lax.rem(block_id, PER)
            key_buf[pl.ds(j * BLK, BLK), :] = near_ref[o, 0, w]
            value_buf[pl.ds(j * BLK, BLK), :] = near_ref[o, 1, w]
        for h in range(q_ref.shape[-1] // HD):
            peak, total, part = softmax_part(b, WIN * BLK, h)
            peak_buf[b, h] = jnp.broadcast_to(peak, (BLK, HD))
            total_buf[b, h] = jnp.broadcast_to(total, (BLK, HD))
            attended_buf[b, :, h * HD:(h + 1) * HD] = part
        return carry

    def rest_part(b, carry):
        for r in range(5):
            slot = b * 3 + r if r < 3 else RANDS + r - 3
            key_buf[pl.ds(r * BLK, BLK), :] = sel_ref[0, slot]
            value_buf[pl.ds(r * BLK, BLK), :] = sel_ref[1, slot]
        squares = jnp.zeros((BLK, HD), jnp.float32)
        for h in range(q_ref.shape[-1] // HD):
            peak, total, part = softmax_part(b, 5 * BLK, h)
            overall = jnp.maximum(peak_buf[b, h], peak)
            before = jnp.exp((peak_buf[b, h] - overall) * HD ** -0.5)
            now = jnp.exp((peak - overall) * HD ** -0.5)
            attended = (attended_buf[b, :, h * HD:(h + 1) * HD] * before + part * now) / (
                total_buf[b, h] * before + total * now)
            squares += attended * attended
            attended_buf[b, :, h * HD:(h + 1) * HD] = attended
        square_buf[b] = squares
        return carry

    for g in range(GROUPS):
        if g * PERIOD <= EARLY:
            y_start(0, g, 1)
        begin(z_copies[g])
    own_ids.wait()
    for i in (1, 2, 3):
        begin(remote(ids_ref, ids_all.at[mx], id_send.at[i - 1], id_recv.at[i - 1], to=x_peer[i]))
    keep_own = []
    for g in range(GROUPS):
        own[g].wait()
        copy = pltpu.make_async_copy(col[g].at[0, my], near_ref.at[2, PARTS[g][0], :, :, lanes(g)],
                                     keep_sem.at[g])
        copy.start()
        keep_own.append(copy)

    x_at = {}
    for g in range(GROUPS):
        for i in range(4):
            x_at.setdefault(PERIOD * g + 4 + X_GAP * i, []).append((g, i))
    for tick in range(max(x_at) + 1):
        for g in range(GROUPS):
            start = max(0, PERIOD * g - EARLY)
            if tick == start:
                if start > 0:
                    y_start(0, g, 1)
                z_copies[g].wait_recv()
                y_start(1, g, 1)
        for g in range(GROUPS):
            t = tick - PERIOD * g
            if 1 <= t <= 4:
                for zz in range(2):
                    y_phase(zz, g, t)
            if t == NEAR_AT:
                for n in range(4):
                    begin(w_copy(g, n))
        if tick == 4:
            for i in (1, 2, 3):
                remote(ids_ref, ids_all.at[wrap(mx - i, NX)], id_send.at[i - 1],
                       id_recv.at[i - 1], to=x_peer[i]).wait_recv()
            to_smem = pltpu.make_async_copy(ids_all, ids_smem, smem_sem.at[1])
            to_smem.start()
            to_smem.wait()
        for g, i in x_at.get(tick, ()):
            x_phase(g, i)
        if tick == max(x_at) - 2 * X_GAP:
            for copy in keep_own:
                copy.wait()
            for g in range(GROUPS):
                for n in range(4):
                    w_copy(g, n).wait_recv()
            lax.fori_loop(0, 2, window_part, 0)
        if tick == max(x_at) - X_GAP:
            lax.fori_loop(2, PER, window_part, 0)

    lax.fori_loop(0, PER, rest_part, 0)
    sums[me] = lax.dot_general(
        jnp.ones((8, HD), jnp.float32), square_buf[...].reshape(PER * BLK, HD),
        (((1,), (1,)), ((), ())),
        precision=lax.Precision.HIGHEST, preferred_element_type=jnp.float32)
    for i, peer in enumerate(head_peers):
        begin(remote_copy(sums.at[me], sums.at[me], head_send.at[i], head_recv.at[i], "head", peer))
    for i in range(heads - 1):
        source = lax.rem(me + heads - 1 - i, heads)
        remote_copy(sums.at[source], sums.at[source], head_send.at[i], head_recv.at[i], "head",
                    head_peers[i]).wait_recv()
    total = sums[0]
    for i in range(1, heads):
        total += sums[i]
    inverse = jnp.transpose(lax.rsqrt(total / D + 1e-06))[:, :1]
    for b in range(PER):
        rows = slice(b * BLK, (b + 1) * BLK)
        out_ref[rows, :] = (attended_buf[b] * inverse[rows] * gain_ref[...]).astype(out_ref.dtype)
    for copy in sends:
        copy.wait_send()


def exchange(ids, window, keys, values, queries, gain):
    width = keys.shape[-1]
    heads = lax.axis_size("head")
    dma = pltpu.SemaphoreType.DMA
    hbm = pl.BlockSpec(memory_space=pl.ANY)
    vmem = pl.BlockSpec(memory_space=pltpu.VMEM)
    f32 = lambda *shape: pltpu.VMEM(shape, jnp.float32)
    bf16 = lambda *shape: pltpu.VMEM(shape, jnp.bfloat16)
    return pl.pallas_call(
        partial(exchange_kernel, heads),
        out_shape=jax.ShapeDtypeStruct((PER * BLK, width), jnp.bfloat16),
        in_specs=[vmem, pl.BlockSpec(memory_space=pltpu.SMEM), hbm, hbm, vmem, vmem],
        out_specs=vmem,
        scratch_shapes=[
            *[pltpu.VMEM((2, NY, PER, BLK, part[2]), jnp.bfloat16) for part in PARTS],
            *[pltpu.VMEM((2, 3, HALF, BLK, part[2]), jnp.bfloat16) for part in PARTS * 2],
            pltpu.VMEM((NX, 8, 128), jnp.int32),
            pltpu.SMEM((NX, 8, 128), jnp.int32),
            dma((GROUPS,)), dma((GROUPS,)), dma((3,)), dma((3,)), dma((GROUPS,)), dma((GROUPS,)),
            dma((GROUPS, 4)), dma((GROUPS, 4)),
            dma((2, GROUPS, 2, 4)), dma((2, GROUPS, 2, 4)),
            dma((GROUPS, 2, 3)), dma((GROUPS, 2, 3)), dma((2,)),
            bf16(5, 2, PER, BLK, width), bf16(2, SLOTS, BLK, width),
            bf16(WIN * BLK, width), bf16(WIN * BLK, width),
            f32(PER, BLK, width), f32(PER, BLK, HD),
            f32(PER, width // HD, BLK, HD), f32(PER, width // HD, BLK, HD),
            f32(heads, 8, PER * BLK), dma((heads - 1,)), dma((heads - 1,)),
        ],
        compiler_params=pltpu.CompilerParams(
            collective_id=0, has_side_effects=True, vmem_limit_bytes=48 << 20),
        name="exchange",
    )(ids, window, keys, values, queries, gain)


def body(queries, key_rows, value_rows, window, random_blocks, global_blocks, norm_gain):
    width = queries.shape[1]
    blocks = lambda rows: rows.reshape(PER, BLK, width)
    ids = jnp.concatenate([random_blocks.reshape(-1), global_blocks])
    ids = jnp.broadcast_to(jnp.pad(ids, (0, 128 - SLOTS))[None, :], (8, 128))
    return exchange(ids, window, blocks(key_rows), blocks(value_rows), blocks(queries),
                    norm_gain[None, :])


def solution(mesh):
    placed = (
        P("seq", "head"),
        P("seq", "head"),
        P("seq", "head"),
        P("seq", None),
        P("seq", None),
        P(),
        P("head"),
    )
    return jax.shard_map(
        body, mesh=mesh, in_specs=placed, out_specs=P("seq", "head"), check_vma=False
    )
```
